32 devices in a mesh: dp: 4 (over z), expert: 8 (over y, x, core).
Axes of the slice: x: 2, y: 2, z: 4, core: 2. Of those that a mesh axis runs over, the one named last changes fastest.
Arguments:
- tokens: bfloat16 [4096, 2048], P(('dp', 'expert')), may hold values from -6 to 6
- grad_out: bfloat16 [4096, 2048], P(('dp', 'expert')), may hold values from -6 to 6
- combine_weights: bfloat16 [4096, 3], P(('dp', 'expert')), may hold values from 0.099609375 to 1
- expert_ids: int32 [4096, 3], P(('dp', 'expert')), may hold values from 0 to 7, as said below
- w_in: bfloat16 [8, 2048, 1536], P('expert'), may hold values from -0.125 to 0.125
- w_out: bfloat16 [8, 2048, 768], P('expert'), may hold values from -0.21875 to 0.21875
Outputs:
- d_tokens: bfloat16 [4096, 2048], P(('dp', 'expert'))
- d_combine: bfloat16 [4096, 3], P(('dp', 'expert'))
- d_w_in: float32 [8, 2048, 1536], P('expert', 'dp')
- d_w_out: float32 [8, 2048, 768], P('expert', 'dp')
The draws below stay inside these ranges and needn't reach their ends.
Inputs may be any that keep to these rules, and one draw needn't show every extreme that they name: `expert_ids`: each row names 3 different experts; within the 128 rows of one device no expert is named more than 96 times.
All inputs are finite; a program needn't handle non-finite values.
Results may differ from the reference program's by a relative error of at most 0.01.
Values may be sent and summed in bfloat16 or wider, within the bound.
A program may use at most 128 MiB of HBM per device.

```python
import math
import jax
import jax.numpy as jnp
from jax import lax

D = 2048
FF = 768
TOK_DEV = 128
TOP = 3
TILE = 128
EXPERTS = 8
GROUP_TOK = 1024
TOKENS = 4096
CAP = 96


def draw_expert_ids(key, part):
    block_count = TOKENS // TOK_DEV
    group_count = block_count // EXPERTS
    key_hot, key_blocks = jax.random.split(jax.random.fold_in(key, 7))
    hot_group = jax.random.randint(key_hot, (group_count,), 0, EXPERTS).astype(jnp.int32)
    hot_block = jnp.repeat(hot_group, EXPERTS)
    block_keys = jax.random.split(key_blocks, block_count)

    def one_block(block_key, hot_expert):
        key_pool, key_order = jax.random.split(block_key)
        others = jnp.repeat(jnp.arange(EXPERTS - 1, dtype=jnp.int32), CAP)
        others = others + (others >= hot_expert).astype(jnp.int32)
        others = jax.random.permutation(key_pool, others)
        remain = TOK_DEV * TOP - CAP
        sequence = jnp.concatenate([others[:remain], jnp.full((CAP,), 1, jnp.int32) * hot_expert])
        sequence = jnp.sort(sequence)
        chosen = sequence.reshape(TOP, TOK_DEV).T
        order = jax.random.permutation(key_order, TOK_DEV)
        return chosen[order]
    result = jax.vmap(one_block)(block_keys, hot_block)
    return result.reshape(TOKENS, TOP).astype(jnp.int32)


def shard_levels(stream_key, extent, shards, smallest, top_value):
    level, own = 1.0, jax.random.fold_in(stream_key, 6)
    for position, parts in shards:
        steps = jnp.exp(jax.random.uniform(jax.random.fold_in(own, position), (parts,), jnp.float32, smallest / len(shards), top_value / len(shards)))
        level = level * jnp.repeat(steps, extent[position] // parts).reshape([-1 if axis == position else 1 for axis in range(len(extent))])
    return level


def gaussian(rng, extent, deviation, most, pieces=(), kind=jnp.bfloat16):
    entries = jax.random.normal(rng, extent, jnp.float32) * deviation
    if len(pieces) > 0:
        entries = shard_levels(rng, extent, pieces, -0.22, 0.18) * entries
    return jnp.clip(entries, min=-most, max=most).astype(kind)


def setup_inputs(seed: int = 0) -> dict:
    keys = jax.random.split(jax.random.key(seed), 7)
    tokens = gaussian(keys[0], (TOKENS, D), 1.0, 6.0, ((0, 32),))
    grad_out = gaussian(keys[1], (TOKENS, D), 1.0, 6.0, ((0, 32),))
    combine_weights = jnp.clip(jnp.exp(math.log(1.0) - 2.306499 * jax.random.uniform(keys[2], (TOKENS, TOP), jnp.float32) ** shard_levels(keys[2], (TOKENS, TOP), ((0, 32),), -0.2, 0.2)), 0.099609375, 1.0).astype(jnp.bfloat16)
    expert_ids = draw_expert_ids(jax.random.fold_in(keys[6], 71), 0)
    w_in = gaussian(keys[4], (EXPERTS, D, 2 * FF), D ** -0.5, 0.125, ((0, 8),))
    w_out = gaussian(keys[5], (EXPERTS, D, FF), FF ** -0.5, 0.21875, ((0, 8),))
    return dict(tokens=tokens, grad_out=grad_out, combine_weights=combine_weights, expert_ids=expert_ids, w_in=w_in, w_out=w_out)


def rows_backward(x_rows, dy_rows, p_rows, w_in_e, w_out_e):
    hidden_width = w_out_e.shape[1]
    gate_up = jnp.dot(x_rows, w_in_e, preferred_element_type=jnp.float32)
    gate_pre = gate_up[:, :hidden_width]
    up_pre = gate_up[:, hidden_width:]
    sigmoid_gate = jax.nn.sigmoid(gate_pre)
    gate_act = gate_pre * sigmoid_gate
    hidden = (gate_act * up_pre).astype(jnp.bfloat16)
    output = jnp.dot(hidden, w_out_e.T, preferred_element_type=jnp.float32)
    d_prob = jnp.sum(dy_rows.astype(jnp.float32) * output, axis=1)
    d_output = (p_rows.astype(jnp.float32)[:, None] * dy_rows.astype(jnp.float32)).astype(jnp.bfloat16)
    d_hidden = jnp.dot(d_output, w_out_e, preferred_element_type=jnp.float32)
    d_gate = d_hidden * up_pre * (sigmoid_gate * (1.0 + gate_pre * (1.0 - sigmoid_gate)))
    d_up = d_hidden * gate_act
    d_gate_up = jnp.concatenate([d_gate, d_up], axis=1).astype(jnp.bfloat16)
    d_rows = jnp.dot(d_gate_up, w_in_e.T, preferred_element_type=jnp.float32).astype(jnp.bfloat16)
    return d_rows, d_prob, d_gate_up, d_output, hidden


def reference(tokens, grad_out, combine_weights, expert_ids, w_in, w_out):
    group_count = TOKENS // GROUP_TOK
    slot_count = GROUP_TOK * TOP
    tile_count = slot_count // TILE + EXPERTS + 1
    padded_rows = tile_count * TILE

    def group_pass(total, group_index):
        first = (group_index * GROUP_TOK).astype(jnp.int32)
        x_group = lax.dynamic_slice_in_dim(tokens, first, GROUP_TOK, 0)
        dy_group = lax.dynamic_slice_in_dim(grad_out, first, GROUP_TOK, 0)
        p_group = lax.dynamic_slice_in_dim(combine_weights, first, GROUP_TOK, 0).reshape(-1)
        ids_flat = lax.dynamic_slice_in_dim(expert_ids, first, GROUP_TOK, 0).reshape(-1)
        one_hot = (ids_flat[:, None] == jnp.arange(EXPERTS, dtype=jnp.int32)[None, :]).astype(jnp.int32)
        counts = jnp.sum(one_hot, axis=0)
        earlier = jnp.cumsum(one_hot, axis=0) - one_hot
        rank = jnp.sum(earlier * one_hot, axis=1)
        padded = ((counts + TILE - 1) // TILE) * TILE
        pad_start = jnp.cumsum(padded) - padded
        target = (jnp.take(pad_start, ids_flat) + rank).astype(jnp.int32)
        source = jnp.full((padded_rows,), slot_count, jnp.int32).at[target].set(jnp.arange(slot_count, dtype=jnp.int32))
        tile_first = jnp.arange(tile_count, dtype=jnp.int32) * TILE
        tile_expert = jnp.minimum(jnp.sum((tile_first[:, None] >= (pad_start + padded)[None, :]).astype(jnp.int32), axis=1), EXPERTS - 1)
        valid = source < slot_count
        safe = jnp.minimum(source, slot_count - 1)
        owner = safe // TOP
        x_rows = jnp.where(valid[:, None], x_group[owner], jnp.zeros((), tokens.dtype))
        dy_rows = jnp.where(valid[:, None], dy_group[owner], jnp.zeros((), grad_out.dtype))
        p_rows = jnp.where(valid, p_group[safe], jnp.zeros((), combine_weights.dtype))
        x_tiles = x_rows.reshape(tile_count, TILE, D)
        dy_tiles = dy_rows.reshape(tile_count, TILE, D)
        p_tiles = p_rows.reshape(tile_count, TILE)

        def tile_pass(accum, item):
            x_tile, dy_tile, p_tile, expert_now = item
            w_in_e = w_in[expert_now]
            w_out_e = w_out[expert_now]
            d_rows, d_prob, d_gate_up, d_output, hidden = rows_backward(x_tile, dy_tile, p_tile, w_in_e, w_out_e)
            term_in = jnp.dot(x_tile.T, d_gate_up, preferred_element_type=jnp.float32)
            term_out = jnp.dot(d_output.T, hidden, preferred_element_type=jnp.float32)
            accum = accum.at[expert_now].add(jnp.concatenate([term_in, term_out], axis=1))
            return accum, (d_rows, d_prob)

        accum_start = jnp.zeros((EXPERTS, D, 3 * FF), jnp.float32)
        accum, (d_rows, d_prob) = lax.scan(tile_pass, accum_start, (x_tiles, dy_tiles, p_tiles, tile_expert))
        rounded = lax.optimization_barrier(accum.astype(jnp.bfloat16))
        total = total + rounded.astype(jnp.float32)
        d_slot = d_rows.reshape(padded_rows, D)[target]
        d_tok = jnp.sum(d_slot.reshape(GROUP_TOK, TOP, D).astype(jnp.float32), axis=1).astype(jnp.bfloat16)
        d_comb = d_prob.reshape(padded_rows)[target].reshape(GROUP_TOK, TOP).astype(jnp.bfloat16)
        return total, (d_tok, d_comb)

    total_start = jnp.zeros((EXPERTS, D, 3 * FF), jnp.float32)
    total, (d_tok, d_comb) = lax.scan(group_pass, total_start, jnp.arange(group_count, dtype=jnp.int32))
    d_tokens = d_tok.reshape(TOKENS, D)
    d_combine = d_comb.reshape(TOKENS, TOP)
    return d_tokens, d_combine, total[:, :, :2 * FF], total[:, :, 2 * FF:]
```

```python
import jax
import jax.numpy as jnp
from jax import lax
from jax.sharding import PartitionSpec as P


def dot_rows(lhs, rhs):
    return lax.dot_general(lhs, rhs, (((0,), (0,)), ((), ())), preferred_element_type=jnp.float32)


def scatter_sum(part):
    return lax.psum_scatter(
        part.astype(jnp.bfloat16), "dp", scatter_dimension=0, tiled=True
    ).astype(jnp.float32)


def body(tokens, grad_out, combine_weights, expert_ids, w_in, w_out):
    experts = lax.axis_size("expert")
    tok_rows, routed = expert_ids.shape
    model_width = tokens.shape[1]
    hidden_width = w_out.shape[2]
    w_in_e = w_in[0]
    w_out_e = w_out[0]

    named = expert_ids[None, :, :] == jnp.arange(experts, dtype=jnp.int32)[:, None, None]
    dense_p = jnp.sum(jnp.where(named, combine_weights[None].astype(jnp.float32), 0.0), axis=2)
    p_rows = lax.all_to_all(
        dense_p.astype(jnp.bfloat16), "expert", split_axis=0, concat_axis=0, tiled=True
    )
    p_rows = p_rows.reshape(experts * tok_rows)[:, None].astype(jnp.float32)

    x_rows = lax.all_gather(tokens, "expert", axis=0, tiled=True)
    dy_rows = lax.all_gather(grad_out, "expert", axis=0, tiled=True)

    gate_up = jnp.dot(x_rows, w_in_e, preferred_element_type=jnp.float32)
    gate_pre = gate_up[:, :hidden_width]
    up_pre = gate_up[:, hidden_width:]
    sigmoid_gate = jax.nn.sigmoid(gate_pre)
    gate_act = gate_pre * sigmoid_gate
    hidden = (gate_act * up_pre).astype(jnp.bfloat16)

    d_output = (p_rows * dy_rows.astype(jnp.float32)).astype(jnp.bfloat16)
    d_w_out = scatter_sum(dot_rows(d_output, hidden))

    dy_hidden = jnp.dot(dy_rows, w_out_e, preferred_element_type=jnp.float32)
    d_prob = jnp.sum(hidden.astype(jnp.float32) * dy_hidden, axis=1)
    d_hidden = p_rows * dy_hidden
    d_gate = d_hidden * up_pre * (sigmoid_gate * (1.0 + gate_pre * (1.0 - sigmoid_gate)))
    d_up = d_hidden * gate_act
    d_gate_up = jnp.concatenate([d_gate, d_up], axis=1).astype(jnp.bfloat16)
    d_w_in = scatter_sum(dot_rows(x_rows, d_gate_up))

    d_rows = lax.dot_general(
        d_gate_up, w_in_e, (((1,), (1,)), ((), ())), preferred_element_type=jnp.float32
    ).astype(jnp.bfloat16)
    back_rows = lax.all_to_all(
        d_rows.reshape(experts, tok_rows, model_width),
        "expert",
        split_axis=0,
        concat_axis=0,
        tiled=True,
    )
    back_prob = lax.all_to_all(
        d_prob.astype(jnp.bfloat16).reshape(experts, tok_rows),
        "expert",
        split_axis=0,
        concat_axis=0,
        tiled=True,
    )
    d_tokens = jnp.sum(back_rows.astype(jnp.float32), axis=0).astype(jnp.bfloat16)
    d_combine = jnp.sum(
        jnp.where(named, back_prob.astype(jnp.float32)[:, :, None], 0.0), axis=0
    ).astype(jnp.bfloat16)
    return (d_tokens, d_combine, d_w_in[None], d_w_out[None])


def solution(mesh):
    placed = (
        P(("dp", "expert"), None),
        P(("dp", "expert"), None),
        P(("dp", "expert"), None),
        P(("dp", "expert"), None),
        P("expert", None, None),
        P("expert", None, None),
    )
    return jax.shard_map(
        body,
        mesh=mesh,
        in_specs=placed,
        out_specs=(
            P(("dp", "expert"), None),
            P(("dp", "expert"), None),
            P("expert", "dp", None),
            P("expert", "dp", None),
        ),
        check_vma=False,
    )
```

```python
import jax
import jax.numpy as jnp
from jax import lax
from jax.experimental import pallas as pl
from jax.experimental.layout import Layout, with_layout_constraint
from jax.experimental.pallas import tpu as pltpu
from jax.sharding import PartitionSpec as P

MESH = pl.DeviceIdType.MESH


def flipped(index, stride):
    return index + stride - 2 * stride * ((index // stride) % 2)


def gather_kernel(
    x_ref, dy_ref, p_ref, x_all, dy_all, p_all, send_sem, recv_sem, p_send, p_recv, local_sem
):
    devices = p_all.shape[0]
    tok_rows = x_ref.shape[0]
    me = lax.axis_index("expert")
    core, side, up = flipped(me, 1), flipped(me, 2), flipped(me, 4)
    across = flipped(side, 4)
    alls = (x_all, dy_all)

    barrier = pltpu.get_barrier_semaphore()
    for step in range(1, devices):
        pl.semaphore_signal(
            barrier,
            inc=1,
            device_id={"expert": lax.rem(me + step, devices)},
            device_id_type=MESH,
        )
    pl.semaphore_wait(barrier, devices - 1)

    started = []

    def block(array, owner):
        return alls[array].at[pl.ds(pl.multiple_of(owner * tok_rows, tok_rows), tok_rows)]

    def send(src, array, owner, target):
        copy = pltpu.make_async_remote_copy(
            src_ref=src,
            dst_ref=block(array, owner),
            send_sem=send_sem.at[len(started)],
            recv_sem=recv_sem.at[array, owner],
            device_id={"expert": target},
            device_id_type=MESH,
        )
        copy.start()
        started.append(copy)

    def arrived(array, owner):
        pltpu.make_async_remote_copy(
            src_ref=block(array, owner),
            dst_ref=block(array, owner),
            send_sem=send_sem.at[0],
            recv_sem=recv_sem.at[array, owner],
            device_id={"expert": core},
            device_id_type=MESH,
        ).wait_recv()

    p_copies = []
    for step in range(1, devices):
        copy = pltpu.make_async_remote_copy(
            src_ref=p_ref,
            dst_ref=p_all.at[me],
            send_sem=p_send.at[step],
            recv_sem=p_recv.at[me],
            device_id={"expert": lax.rem(me + step, devices)},
            device_id_type=MESH,
        )
        copy.start()
        p_copies.append(copy)

    send(x_ref, 0, me, side)
    send(dy_ref, 1, me, up)
    send(dy_ref, 1, me, side)
    send(x_ref, 0, me, up)
    send(x_ref, 0, me, core)
    send(dy_ref, 1, me, core)

    own = (
        pltpu.make_async_copy(x_ref, block(0, me), local_sem.at[0]),
        pltpu.make_async_copy(dy_ref, block(1, me), local_sem.at[1]),
        pltpu.make_async_copy(p_ref, p_all.at[me], local_sem.at[2]),
    )
    for copy in own:
        copy.start()

    def relay(array, owner, targets):
        arrived(array, owner)
        for target in targets:
            send(block(array, owner), array, owner, target)

    relay(0, side, (up, core))
    relay(1, up, (side, core))
    relay(1, side, (core,))
    relay(0, up, (core,))
    relay(0, across, (core,))
    relay(1, across, (core,))

    for array in range(2):
        for owner in (core, flipped(core, 2), flipped(core, 4), flipped(across, 1)):
            arrived(array, owner)
    for step in range(1, devices):
        owner = lax.rem(me + step, devices)
        pltpu.make_async_remote_copy(
            src_ref=p_ref,
            dst_ref=p_all.at[owner],
            send_sem=p_send.at[step],
            recv_sem=p_recv.at[owner],
            device_id={"expert": owner},
            device_id_type=MESH,
        ).wait_recv()
    for copy in started + p_copies:
        copy.wait_send()
    for copy in own:
        copy.wait()


def gather_all(tokens, grad_out, dense_p, devices):
    if devices != 8:
        return tuple(
            lax.all_gather(array, "expert", axis=0, tiled=tiled)
            for array, tiled in ((tokens, True), (grad_out, True), (dense_p, False))
        )
    tok_rows, model_width = tokens.shape
    whole = jax.ShapeDtypeStruct((devices * tok_rows, model_width), tokens.dtype)
    return pl.pallas_call(
        gather_kernel,
        out_shape=(
            whole,
            whole,
            jax.ShapeDtypeStruct((devices,) + dense_p.shape, dense_p.dtype),
        ),
        in_specs=[pl.BlockSpec(memory_space=pltpu.VMEM)] * 3,
        out_specs=(
            pl.BlockSpec(memory_space=pl.ANY),
            pl.BlockSpec(memory_space=pl.ANY),
            pl.BlockSpec(memory_space=pltpu.VMEM),
        ),
        scratch_shapes=[
            pltpu.SemaphoreType.DMA((14,)),
            pltpu.SemaphoreType.DMA((2, devices)),
            pltpu.SemaphoreType.DMA((devices,)),
            pltpu.SemaphoreType.DMA((devices,)),
            pltpu.SemaphoreType.DMA((3,)),
        ],
        compiler_params=pltpu.CompilerParams(collective_id=0, has_side_effects=True),
    )(tokens, grad_out, dense_p)


def dot_rows(lhs, rhs):
    return lax.dot_general(lhs, rhs, (((0,), (0,)), ((), ())), preferred_element_type=jnp.float32)


def row_major(array):
    return with_layout_constraint(array, Layout(major_to_minor=(0, 1)))


def scatter_sum(part):
    return lax.psum_scatter(part, "dp", scatter_dimension=0, tiled=True).astype(jnp.float32)


def body(tokens, grad_out, combine_weights, expert_ids, w_in, w_out):
    experts = lax.axis_size("expert")
    tok_rows, routed = expert_ids.shape
    model_width = tokens.shape[1]
    hidden_width = w_out.shape[2]
    w_in_e = w_in[0]
    w_out_e = w_out[0]

    named = expert_ids[None, :, :] == jnp.arange(experts, dtype=jnp.int32)[:, None, None]
    dense_p = jnp.sum(jnp.where(named, combine_weights[None].astype(jnp.float32), 0.0), axis=2)
    x_rows, dy_rows, p_all = gather_all(tokens, grad_out, dense_p, experts)
    p_rows = lax.dynamic_index_in_dim(p_all, lax.axis_index("expert"), 1, keepdims=False)
    p_rows = p_rows.reshape(experts * tok_rows)[:, None]

    gate_up = jnp.dot(x_rows, w_in_e, preferred_element_type=jnp.float32)
    gate_pre = gate_up[:, :hidden_width]
    up_pre = gate_up[:, hidden_width:]
    sigmoid_gate = jax.nn.sigmoid(gate_pre)
    gate_act = gate_pre * sigmoid_gate
    hidden = lax.optimization_barrier((gate_act * up_pre).astype(jnp.bfloat16))

    d_output = (p_rows * dy_rows.astype(jnp.float32)).astype(jnp.bfloat16)
    part_out, dy_rows = lax.optimization_barrier(
        (row_major(dot_rows(d_output, hidden).astype(jnp.bfloat16)), dy_rows)
    )
    d_w_out = scatter_sum(part_out)

    dy_hidden = jnp.dot(dy_rows, w_out_e, preferred_element_type=jnp.float32)
    d_prob = jnp.sum(hidden.astype(jnp.float32) * dy_hidden, axis=1)
    d_hidden = p_rows * dy_hidden
    d_gate = d_hidden * up_pre * (sigmoid_gate * (1.0 + gate_pre * (1.0 - sigmoid_gate)))
    d_up = d_hidden * gate_act
    d_gate_up = jnp.concatenate([d_gate, d_up], axis=1).astype(jnp.bfloat16)
    part_in, d_prob, d_gate_up = lax.optimization_barrier(
        (row_major(dot_rows(x_rows, d_gate_up).astype(jnp.bfloat16)), d_prob, d_gate_up)
    )
    d_w_in = scatter_sum(part_in)

    d_rows = lax.dot_general(
        d_gate_up, w_in_e, (((1,), (1,)), ((), ())), preferred_element_type=jnp.float32
    ).astype(jnp.bfloat16)
    back_rows = lax.all_to_all(
        d_rows.reshape(experts, tok_rows, model_width),
        "expert",
        split_axis=0,
        concat_axis=0,
        tiled=True,
    )
    back_prob = lax.all_to_all(
        d_prob.astype(jnp.bfloat16).reshape(experts, tok_rows),
        "expert",
        split_axis=0,
        concat_axis=0,
        tiled=True,
    )
    d_tokens = jnp.sum(back_rows.astype(jnp.float32), axis=0).astype(jnp.bfloat16)
    d_combine = jnp.sum(
        jnp.where(named, back_prob.astype(jnp.float32)[:, :, None], 0.0), axis=0
    ).astype(jnp.bfloat16)
    return (d_tokens, d_combine, d_w_in[None], d_w_out[None])


def solution(mesh):
    placed = (
        P(("dp", "expert"), None),
        P(("dp", "expert"), None),
        P(("dp", "expert"), None),
        P(("dp", "expert"), None),
        P("expert", None, None),
        P("expert", None, None),
    )
    return jax.shard_map(
        body,
        mesh=mesh,
        in_specs=placed,
        out_specs=(
            P(("dp", "expert"), None),
            P(("dp", "expert"), None),
            P("expert", "dp", None),
            P("expert", "dp", None),
        ),
        check_vma=False,
    )
```

```python
import jax
import jax.numpy as jnp
from jax import lax
from jax.experimental import pallas as pl
from jax.experimental.layout import Layout, with_layout_constraint
from jax.experimental.pallas import tpu as pltpu
from jax.sharding import PartitionSpec as P

MESH = pl.DeviceIdType.MESH


def flipped(index, stride):
    return index + stride - 2 * stride * ((index // stride) % 2)


def gather_kernel(
    x_ref, dy_ref, p_ref, w_ref, x_all, dy_all, p_all, gate_all, hidden_all,
    x_buf, w_buf, gate_buf, hidden_buf,
    send_sem, recv_sem, half_sem, p_send, p_recv, local_sem, load_sem, out_sem,
):
    devices = p_all.shape[0]
    tok_rows = x_ref.shape[0]
    me = lax.axis_index("expert")
    core, side, up = flipped(me, 1), flipped(me, 2), flipped(me, 4)
    across = flipped(side, 4)
    alls = (x_all, dy_all)

    barrier = pltpu.get_barrier_semaphore()
    for step in range(1, devices):
        pl.semaphore_signal(
            barrier,
            inc=1,
            device_id={"expert": lax.rem(me + step, devices)},
            device_id_type=MESH,
        )
    pl.semaphore_wait(barrier, devices - 1)

    started = []

    half = tok_rows // 2
    hidden_width = hidden_all.shape[1]

    def block(array, owner, part=None):
        if part is None:
            return alls[array].at[pl.ds(pl.multiple_of(owner * tok_rows, tok_rows), tok_rows)]
        first = pl.multiple_of(owner * tok_rows + part * half, half)
        return alls[array].at[pl.ds(first, half)]

    def arrival_sem(array, owner, part):
        return recv_sem.at[array, owner] if part is None else half_sem.at[array, part]

    def send(src, array, owner, target, part=None):
        copy = pltpu.make_async_remote_copy(
            src_ref=src,
            dst_ref=block(array, owner, part),
            send_sem=send_sem.at[len(started)],
            recv_sem=arrival_sem(array, owner, part),
            device_id={"expert": target},
            device_id_type=MESH,
        )
        copy.start()
        started.append(copy)

    def arrived(array, owner, part=None):
        pltpu.make_async_remote_copy(
            src_ref=block(array, owner, part),
            dst_ref=block(array, owner, part),
            send_sem=send_sem.at[0],
            recv_sem=arrival_sem(array, owner, part),
            device_id={"expert": core},
            device_id_type=MESH,
        ).wait_recv()

    p_copies = []
    for step in range(1, devices):
        copy = pltpu.make_async_remote_copy(
            src_ref=p_ref,
            dst_ref=p_all.at[me],
            send_sem=p_send.at[step],
            recv_sem=p_recv.at[me],
            device_id={"expert": lax.rem(me + step, devices)},
            device_id_type=MESH,
        )
        copy.start()
        p_copies.append(copy)

    for array, src in enumerate((x_ref, dy_ref)):
        send(src, array, me, side)
        send(src, array, me, up)
        send(src, array, me, core)

    own = (
        pltpu.make_async_copy(x_ref, block(0, me), local_sem.at[0]),
        pltpu.make_async_copy(dy_ref, block(1, me), local_sem.at[1]),
        pltpu.make_async_copy(p_ref, p_all.at[me], local_sem.at[2]),
    )
    for copy in own:
        copy.start()

    weights = pltpu.make_async_copy(w_ref, w_buf, load_sem.at[0])
    weights.start()
    outs = []

    def pass_on(array):
        arrived(array, side)
        send(block(array, side, 0), array, side, up, 0)
        arrived(array, up)
        send(block(array, up, 1), array, up, side, 1)
        send(block(array, side), array, side, core)
        send(block(array, up), array, up, core)

    def pass_across(array):
        arrived(array, across, 0)
        arrived(array, across, 1)
        send(block(array, across), array, across, core)

    def compute(stage, owner):
        rows = pl.ds(pl.multiple_of((owner // 2) * 2 * tok_rows, 2 * tok_rows), 2 * tok_rows)
        load = pltpu.make_async_copy(x_all.at[rows], x_buf, load_sem.at[1])
        load.start()
        load.wait()

        def tile(j, carry):
            gate_cols = pl.ds(pl.multiple_of(j * 256, 256), 256)
            up_cols = pl.ds(pl.multiple_of(hidden_width + j * 256, 256), 256)
            a = jnp.dot(x_buf[...], w_buf[:, gate_cols], preferred_element_type=jnp.float32)
            b = jnp.dot(x_buf[...], w_buf[:, up_cols], preferred_element_type=jnp.float32)
            gate_buf[stage, :, gate_cols] = a
            gate_buf[stage, :, up_cols] = b
            hidden_buf[stage, :, gate_cols] = (a * jax.nn.sigmoid(a) * b).astype(jnp.bfloat16)
            return carry

        lax.fori_loop(0, hidden_width // 256, tile, 0)
        for copy in (
            pltpu.make_async_copy(gate_buf.at[stage], gate_all.at[rows], out_sem.at[stage, 0]),
            pltpu.make_async_copy(hidden_buf.at[stage], hidden_all.at[rows], out_sem.at[stage, 1]),
        ):
            copy.start()
            outs.append(copy)

    own[0].wait()
    arrived(0, core)
    weights.wait()
    compute(0, me)
    pass_on(0)
    arrived(0, flipped(side, 1))
    compute(1, side)
    pass_on(1)
    arrived(0, flipped(up, 1))
    compute(2, up)
    pass_across(0)
    arrived(0, flipped(across, 1))
    compute(3, across)
    pass_across(1)

    for owner in (core, flipped(side, 1), flipped(up, 1), flipped(across, 1)):
        arrived(1, owner)
    for step in range(1, devices):
        owner = lax.rem(me + step, devices)
        pltpu.make_async_remote_copy(
            src_ref=p_ref,
            dst_ref=p_all.at[owner],
            send_sem=p_send.at[step],
            recv_sem=p_recv.at[owner],
            device_id={"expert": owner},
            device_id_type=MESH,
        ).wait_recv()
    for copy in started + p_copies:
        copy.wait_send()
    for copy in own[1:]:
        copy.wait()
    for copy in outs:
        copy.wait()


def gate_hidden(gate_up):
    hidden_width = gate_up.shape[1] // 2
    gate_pre = gate_up[:, :hidden_width]
    return (gate_pre * jax.nn.sigmoid(gate_pre) * gate_up[:, hidden_width:]).astype(jnp.bfloat16)


def gather_all(tokens, grad_out, dense_p, w_in_e, devices):
    tok_rows, model_width = tokens.shape
    hidden_width = w_in_e.shape[1] // 2
    if devices != 8:
        x_rows, dy_rows, p_all = (
            lax.all_gather(array, "expert", axis=0, tiled=tiled)
            for array, tiled in ((tokens, True), (grad_out, True), (dense_p, False))
        )
        gate_up = jnp.dot(x_rows, w_in_e, preferred_element_type=jnp.float32)
        return x_rows, dy_rows, p_all, gate_up, lax.optimization_barrier(gate_hidden(gate_up))
    whole = jax.ShapeDtypeStruct((devices * tok_rows, model_width), tokens.dtype)
    return pl.pallas_call(
        gather_kernel,
        out_shape=(
            whole,
            whole,
            jax.ShapeDtypeStruct((devices,) + dense_p.shape, dense_p.dtype),
            jax.ShapeDtypeStruct((devices * tok_rows, 2 * hidden_width), jnp.float32),
            jax.ShapeDtypeStruct((devices * tok_rows, hidden_width), jnp.bfloat16),
        ),
        in_specs=[pl.BlockSpec(memory_space=pltpu.VMEM)] * 3 + [pl.BlockSpec(memory_space=pl.ANY)],
        out_specs=(
            pl.BlockSpec(memory_space=pl.ANY),
            pl.BlockSpec(memory_space=pl.ANY),
            pl.BlockSpec(memory_space=pltpu.VMEM),
            pl.BlockSpec(memory_space=pl.ANY),
            pl.BlockSpec(memory_space=pl.ANY),
        ),
        scratch_shapes=[
            pltpu.VMEM((2 * tok_rows, model_width), tokens.dtype),
            pltpu.VMEM(w_in_e.shape, w_in_e.dtype),
            pltpu.VMEM((devices // 2, 2 * tok_rows, 2 * hidden_width), jnp.float32),
            pltpu.VMEM((devices // 2, 2 * tok_rows, hidden_width), jnp.bfloat16),
            pltpu.SemaphoreType.DMA((16,)),
            pltpu.SemaphoreType.DMA((2, devices)),
            pltpu.SemaphoreType.DMA((2, 2)),
            pltpu.SemaphoreType.DMA((devices,)),
            pltpu.SemaphoreType.DMA((devices,)),
            pltpu.SemaphoreType.DMA((3,)),
            pltpu.SemaphoreType.DMA((2,)),
            pltpu.SemaphoreType.DMA((devices // 2, 2)),
        ],
        compiler_params=pltpu.CompilerParams(
            collective_id=0, has_side_effects=True, vmem_limit_bytes=60 * 1024 * 1024
        ),
    )(tokens, grad_out, dense_p, w_in_e)


def dot_rows(lhs, rhs):
    return lax.dot_general(lhs, rhs, (((0,), (0,)), ((), ())), preferred_element_type=jnp.float32)


def row_major(array):
    return with_layout_constraint(array, Layout(major_to_minor=(0, 1)))


def scatter_sum(part):
    return lax.psum_scatter(part, "dp", scatter_dimension=0, tiled=True).astype(jnp.float32)


def body(tokens, grad_out, combine_weights, expert_ids, w_in, w_out):
    experts = lax.axis_size("expert")
    tok_rows, routed = expert_ids.shape
    model_width = tokens.shape[1]
    hidden_width = w_out.shape[2]
    w_in_e = w_in[0]
    w_out_e = w_out[0]

    named = expert_ids[None, :, :] == jnp.arange(experts, dtype=jnp.int32)[:, None, None]
    dense_p = jnp.sum(jnp.where(named, combine_weights[None].astype(jnp.float32), 0.0), axis=2)
    x_rows, dy_rows, p_all, gate_up, hidden = gather_all(
        tokens, grad_out, dense_p, w_in_e, experts
    )
    p_rows = lax.dynamic_index_in_dim(p_all, lax.axis_index("expert"), 1, keepdims=False)
    p_rows = p_rows.reshape(experts * tok_rows)[:, None]

    gate_pre = gate_up[:, :hidden_width]
    up_pre = gate_up[:, hidden_width:]
    sigmoid_gate = jax.nn.sigmoid(gate_pre)
    gate_act = gate_pre * sigmoid_gate

    d_output = (p_rows * dy_rows.astype(jnp.float32)).astype(jnp.bfloat16)
    part_out, dy_rows = lax.optimization_barrier(
        (row_major(dot_rows(d_output, hidden).astype(jnp.bfloat16)), dy_rows)
    )
    d_w_out = scatter_sum(part_out)

    dy_hidden = jnp.dot(dy_rows, w_out_e, preferred_element_type=jnp.float32)
    d_prob = jnp.sum(hidden.astype(jnp.float32) * dy_hidden, axis=1)
    d_hidden = p_rows * dy_hidden
    d_gate = d_hidden * up_pre * (sigmoid_gate * (1.0 + gate_pre * (1.0 - sigmoid_gate)))
    d_up = d_hidden * gate_act
    d_gate_up = jnp.concatenate([d_gate, d_up], axis=1).astype(jnp.bfloat16)
    part_in, d_prob, d_gate_up = lax.optimization_barrier(
        (row_major(dot_rows(x_rows, d_gate_up).astype(jnp.bfloat16)), d_prob, d_gate_up)
    )
    d_w_in = scatter_sum(part_in)

    d_rows = lax.dot_general(
        d_gate_up, w_in_e, (((1,), (1,)), ((), ())), preferred_element_type=jnp.float32
    ).astype(jnp.bfloat16)
    back_rows = lax.all_to_all(
        d_rows.reshape(experts, tok_rows, model_width),
        "expert",
        split_axis=0,
        concat_axis=0,
        tiled=True,
    )
    back_prob = lax.all_to_all(
        d_prob.astype(jnp.bfloat16).reshape(experts, tok_rows),
        "expert",
        split_axis=0,
        concat_axis=0,
        tiled=True,
    )
    d_tokens = jnp.sum(back_rows.astype(jnp.float32), axis=0).astype(jnp.bfloat16)
    d_combine = jnp.sum(
        jnp.where(named, back_prob.astype(jnp.float32)[:, :, None], 0.0), axis=0
    ).astype(jnp.bfloat16)
    return (d_tokens, d_combine, d_w_in[None], d_w_out[None])


def solution(mesh):
    placed = (
        P(("dp", "expert"), None),
        P(("dp", "expert"), None),
        P(("dp", "expert"), None),
        P(("dp", "expert"), None),
        P("expert", None, None),
        P("expert", None, None),
    )
    return jax.shard_map(
        body,
        mesh=mesh,
        in_specs=placed,
        out_specs=(
            P(("dp", "expert"), None),
            P(("dp", "expert"), None),
            P("expert", "dp", None),
            P("expert", "dp", None),
        ),
        check_vma=False,
    )
```

```python
import jax
import jax.numpy as jnp
from jax import lax
from jax.experimental import pallas as pl
from jax.experimental.layout import Layout, with_layout_constraint
from jax.experimental.pallas import tpu as pltpu
from jax.sharding import PartitionSpec as P

MESH = pl.DeviceIdType.MESH


def flipped(index, stride):
    return index + stride - 2 * stride * ((index // stride) % 2)


def gather_kernel(
    x_ref, dy_ref, p_ref, w_ref, x_all, dy_all, p_all, gate_all, hidden_all,
    x_buf, w_buf, gate_buf, hidden_buf,
    send_sem, recv_sem, half_sem, p_send, p_recv, local_sem, load_sem, out_sem,
):
    devices = p_all.shape[0]
    tok_rows = x_ref.shape[0]
    me = lax.axis_index("expert")
    core, side, up = flipped(me, 1), flipped(me, 2), flipped(me, 4)
    across = flipped(side, 4)
    alls = (x_all, dy_all)

    barrier = pltpu.get_barrier_semaphore()
    for step in range(1, devices):
        pl.semaphore_signal(
            barrier,
            inc=1,
            device_id={"expert": lax.rem(me + step, devices)},
            device_id_type=MESH,
        )
    pl.semaphore_wait(barrier, devices - 1)

    started = []

    half = tok_rows // 2
    hidden_width = hidden_all.shape[1]

    def block(array, owner, part=None):
        if part is None:
            return alls[array].at[pl.ds(pl.multiple_of(owner * tok_rows, tok_rows), tok_rows)]
        first = pl.multiple_of(owner * tok_rows + part * half, half)
        return alls[array].at[pl.ds(first, half)]

    def arrival_sem(array, owner, part):
        return recv_sem.at[array, owner] if part is None else half_sem.at[array, part]

    def send(src, array, owner, target, part=None):
        copy = pltpu.make_async_remote_copy(
            src_ref=src,
            dst_ref=block(array, owner, part),
            send_sem=send_sem.at[len(started)],
            recv_sem=arrival_sem(array, owner, part),
            device_id={"expert": target},
            device_id_type=MESH,
        )
        copy.start()
        started.append(copy)

    def arrived(array, owner, part=None):
        pltpu.make_async_remote_copy(
            src_ref=block(array, owner, part),
            dst_ref=block(array, owner, part),
            send_sem=send_sem.at[0],
            recv_sem=arrival_sem(array, owner, part),
            device_id={"expert": core},
            device_id_type=MESH,
        ).wait_recv()

    p_copies = []
    for step in range(1, devices):
        copy = pltpu.make_async_remote_copy(
            src_ref=p_ref,
            dst_ref=p_all.at[me],
            send_sem=p_send.at[step],
            recv_sem=p_recv.at[me],
            device_id={"expert": lax.rem(me + step, devices)},
            device_id_type=MESH,
        )
        copy.start()
        p_copies.append(copy)

    for array, src in enumerate((x_ref, dy_ref)):
        send(src, array, me, side)
        send(src, array, me, up)
        send(src, array, me, core)

    own = (
        pltpu.make_async_copy(x_ref, block(0, me), local_sem.at[0]),
        pltpu.make_async_copy(dy_ref, block(1, me), local_sem.at[1]),
        pltpu.make_async_copy(p_ref, p_all.at[me], local_sem.at[2]),
    )
    for copy in own:
        copy.start()

    weights = pltpu.make_async_copy(w_ref, w_buf, load_sem.at[0])
    weights.start()
    outs = []

    def pass_on(array):
        arrived(array, side)
        send(block(array, side, 0), array, side, up, 0)
        arrived(array, up)
        send(block(array, up, 1), array, up, side, 1)
        send(block(array, side), array, side, core)
        send(block(array, up), array, up, core)

    def pass_across(array):
        arrived(array, across, 0)
        arrived(array, across, 1)
        send(block(array, across), array, across, core)

    def compute(stage, owner):
        rows = pl.ds(pl.multiple_of((owner // 2) * 2 * tok_rows, 2 * tok_rows), 2 * tok_rows)
        load = pltpu.make_async_copy(x_all.at[rows], x_buf, load_sem.at[1])
        load.start()
        load.wait()

        def tile(j, carry):
            gate_cols = pl.ds(pl.multiple_of(j * 256, 256), 256)
            up_cols = pl.ds(pl.multiple_of(hidden_width + j * 256, 256), 256)
            a = jnp.dot(x_buf[...], w_buf[:, gate_cols], preferred_element_type=jnp.float32)
            b = jnp.dot(x_buf[...], w_buf[:, up_cols], preferred_element_type=jnp.float32)
            gate_buf[stage, :, gate_cols] = a
            gate_buf[stage, :, up_cols] = b
            hidden_buf[stage, :, gate_cols] = (a * jax.nn.sigmoid(a) * b).astype(jnp.bfloat16)
            return carry

        lax.fori_loop(0, hidden_width // 256, tile, 0)
        for copy in (
            pltpu.make_async_copy(gate_buf.at[stage], gate_all.at[rows], out_sem.at[stage, 0]),
            pltpu.make_async_copy(hidden_buf.at[stage], hidden_all.at[rows], out_sem.at[stage, 1]),
        ):
            copy.start()
            outs.append(copy)

    own[0].wait()
    arrived(0, core)
    weights.wait()
    compute(0, me)
    pass_on(0)
    arrived(0, flipped(side, 1))
    compute(1, side)
    pass_on(1)
    arrived(0, flipped(up, 1))
    compute(2, up)
    pass_across(0)
    arrived(0, flipped(across, 1))
    compute(3, across)
    pass_across(1)

    for owner in (core, flipped(side, 1), flipped(up, 1), flipped(across, 1)):
        arrived(1, owner)
    for step in range(1, devices):
        owner = lax.rem(me + step, devices)
        pltpu.make_async_remote_copy(
            src_ref=p_ref,
            dst_ref=p_all.at[owner],
            send_sem=p_send.at[step],
            recv_sem=p_recv.at[owner],
            device_id={"expert": owner},
            device_id_type=MESH,
        ).wait_recv()
    for copy in started + p_copies:
        copy.wait_send()
    for copy in own[1:]:
        copy.wait()
    for copy in outs:
        copy.wait()


def gate_hidden(gate_up):
    hidden_width = gate_up.shape[1] // 2
    gate_pre = gate_up[:, :hidden_width]
    return (gate_pre * jax.nn.sigmoid(gate_pre) * gate_up[:, hidden_width:]).astype(jnp.bfloat16)


def gather_all(tokens, grad_out, dense_p, w_in_e, devices):
    tok_rows, model_width = tokens.shape
    hidden_width = w_in_e.shape[1] // 2
    if devices != 8:
        x_rows, dy_rows, p_all = (
            lax.all_gather(array, "expert", axis=0, tiled=tiled)
            for array, tiled in ((tokens, True), (grad_out, True), (dense_p, False))
        )
        gate_up = jnp.dot(x_rows, w_in_e, preferred_element_type=jnp.float32)
        return x_rows, dy_rows, p_all, gate_up, lax.optimization_barrier(gate_hidden(gate_up))
    whole = jax.ShapeDtypeStruct((devices * tok_rows, model_width), tokens.dtype)
    return pl.pallas_call(
        gather_kernel,
        out_shape=(
            whole,
            whole,
            jax.ShapeDtypeStruct((devices,) + dense_p.shape, dense_p.dtype),
            jax.ShapeDtypeStruct((devices * tok_rows, 2 * hidden_width), jnp.float32),
            jax.ShapeDtypeStruct((devices * tok_rows, hidden_width), jnp.bfloat16),
        ),
        in_specs=[pl.BlockSpec(memory_space=pltpu.VMEM)] * 3 + [pl.BlockSpec(memory_space=pl.ANY)],
        out_specs=(
            pl.BlockSpec(memory_space=pl.ANY),
            pl.BlockSpec(memory_space=pl.ANY),
            pl.BlockSpec(memory_space=pltpu.VMEM),
            pl.BlockSpec(memory_space=pl.ANY),
            pl.BlockSpec(memory_space=pl.ANY),
        ),
        scratch_shapes=[
            pltpu.VMEM((2 * tok_rows, model_width), tokens.dtype),
            pltpu.VMEM(w_in_e.shape, w_in_e.dtype),
            pltpu.VMEM((devices // 2, 2 * tok_rows, 2 * hidden_width), jnp.float32),
            pltpu.VMEM((devices // 2, 2 * tok_rows, hidden_width), jnp.bfloat16),
            pltpu.SemaphoreType.DMA((16,)),
            pltpu.SemaphoreType.DMA((2, devices)),
            pltpu.SemaphoreType.DMA((2, 2)),
            pltpu.SemaphoreType.DMA((devices,)),
            pltpu.SemaphoreType.DMA((devices,)),
            pltpu.SemaphoreType.DMA((3,)),
            pltpu.SemaphoreType.DMA((2,)),
            pltpu.SemaphoreType.DMA((devices // 2, 2)),
        ],
        compiler_params=pltpu.CompilerParams(
            collective_id=0, has_side_effects=True, vmem_limit_bytes=60 * 1024 * 1024
        ),
    )(tokens, grad_out, dense_p, w_in_e)


def dot_rows(lhs, rhs):
    return lax.dot_general(lhs, rhs, (((0,), (0,)), ((), ())), preferred_element_type=jnp.float32)


def row_major(array):
    return with_layout_constraint(array, Layout(major_to_minor=(0, 1)))


def scatter_sum(part):
    return lax.psum_scatter(part, "dp", scatter_dimension=0, tiled=True).astype(jnp.float32)


def body(tokens, grad_out, combine_weights, expert_ids, w_in, w_out):
    experts = lax.axis_size("expert")
    tok_rows, routed = expert_ids.shape
    model_width = tokens.shape[1]
    hidden_width = w_out.shape[2]
    w_in_e = w_in[0]
    w_out_e = w_out[0]

    named = expert_ids[None, :, :] == jnp.arange(experts, dtype=jnp.int32)[:, None, None]
    dense_p = jnp.sum(jnp.where(named, combine_weights[None].astype(jnp.float32), 0.0), axis=2)
    x_rows, dy_rows, p_all, gate_up, hidden = gather_all(
        tokens, grad_out, dense_p, w_in_e, experts
    )
    p_rows = lax.dynamic_index_in_dim(p_all, lax.axis_index("expert"), 1, keepdims=False)
    p_rows = p_rows.reshape(experts * tok_rows)[:, None]

    gate_pre = gate_up[:, :hidden_width]
    up_pre = gate_up[:, hidden_width:]
    sigmoid_gate = jax.nn.sigmoid(gate_pre)
    gate_act = gate_pre * sigmoid_gate

    weighted = (p_rows * hidden.astype(jnp.float32)).astype(jnp.bfloat16)
    part_out, dy_rows = lax.optimization_barrier(
        (row_major(dot_rows(dy_rows, weighted).astype(jnp.bfloat16)), dy_rows)
    )
    d_w_out = scatter_sum(part_out)

    dy_hidden = jnp.dot(dy_rows, w_out_e, preferred_element_type=jnp.float32)
    d_prob = jnp.sum(hidden.astype(jnp.float32) * dy_hidden, axis=1)
    d_hidden = p_rows * dy_hidden
    d_gate = d_hidden * up_pre * (sigmoid_gate * (1.0 + gate_pre * (1.0 - sigmoid_gate)))
    d_up = d_hidden * gate_act
    d_gate_up = jnp.concatenate([d_gate, d_up], axis=1).astype(jnp.bfloat16)
    part_in, d_prob, d_gate_up = lax.optimization_barrier(
        (row_major(dot_rows(x_rows, d_gate_up).astype(jnp.bfloat16)), d_prob, d_gate_up)
    )
    d_w_in = scatter_sum(part_in)

    d_rows = lax.dot_general(
        d_gate_up, w_in_e, (((1,), (1,)), ((), ())), preferred_element_type=jnp.float32
    ).astype(jnp.bfloat16)
    back_rows = lax.all_to_all(
        d_rows.reshape(experts, tok_rows, model_width),
        "expert",
        split_axis=0,
        concat_axis=0,
        tiled=True,
    )
    back_prob = lax.all_to_all(
        d_prob.astype(jnp.bfloat16).reshape(experts, tok_rows),
        "expert",
        split_axis=0,
        concat_axis=0,
        tiled=True,
    )
    d_tokens = jnp.sum(back_rows.astype(jnp.float32), axis=0).astype(jnp.bfloat16)
    d_combine = jnp.sum(
        jnp.where(named, back_prob.astype(jnp.float32)[:, :, None], 0.0), axis=0
    ).astype(jnp.bfloat16)
    return (d_tokens, d_combine, d_w_in[None], d_w_out[None])


def solution(mesh):
    placed = (
        P(("dp", "expert"), None),
        P(("dp", "expert"), None),
        P(("dp", "expert"), None),
        P(("dp", "expert"), None),
        P("expert", None, None),
        P("expert", None, None),
    )
    return jax.shard_map(
        body,
        mesh=mesh,
        in_specs=placed,
        out_specs=(
            P(("dp", "expert"), None),
            P(("dp", "expert"), None),
            P("expert", "dp", None),
            P("expert", "dp", None),
        ),
        check_vma=False,
    )
```
